32 devices in a mesh: rel: 4 (over z), dev: 8 (over y, x, core).
Axes of the slice: x: 2, y: 2, z: 4, core: 2. Of those that a mesh axis runs over, the one named last changes fastest.
Arguments:
- src_feat: bfloat16 [4, 2048, 1024], P('rel', 'dev'), may hold values from -6 to 6
- rel_w_in: bfloat16 [4, 1024, 1024], P('rel', 'dev'), may hold values from -0.1875 to 0.1875
- rel_w_out: bfloat16 [4, 1024, 1024], P('rel', 'dev'), may hold values from -0.1875 to 0.1875
- tile_source: int32 [4, 32], P('rel'), may hold values from 0 to 15
- tile_edges: int32 [4, 32, 128], P('rel'), may hold values from 0 to 16383
- tile_count: int32 [4, 32], P('rel'), may hold values from 0 to 128, as said below
- target_feat: bfloat16 [1024, 1024], P(('dev', 'rel')), may hold values from -6 to 6
- norm_gain: float32 [1024], replicated, may hold values from 0.5 to 2
- tgt_w_in: bfloat16 [1024, 2048], P(None, 'rel'), may hold values from -0.1875 to 0.1875
- tgt_w_out: bfloat16 [2048, 1024], P('rel'), may hold values from -0.125 to 0.125
- out_grad: bfloat16 [1024, 1024], P(('dev', 'rel')), may hold values from -6 to 6
Outputs:
- updated: bfloat16 [1024, 1024], P(('dev', 'rel'))
- src_grad: bfloat16 [4, 2048, 1024], P('rel', 'dev')
The draws below stay inside these ranges and needn't reach their ends.
Inputs may be any that keep to these rules, and one draw needn't show every extreme that they name: Tile k of a relation joins target rows 128 * (k // 4) onward with source rows 128 * tile_source onward. `tile_edges`: each entry is t * 128 + s for an edge from in-tile source offset s to in-tile target offset t; entries past a tile's count are ignored; the same edge may stand several times. The first tile_count entries of a tile's row of tile_edges are its edges; 0 marks an empty tile; in every relation some tile holds 128 edges.
All inputs are finite; a program needn't handle non-finite values.
Results may differ from the reference program's by a relative error of at most 0.013.
Values may be sent and summed in bfloat16 or wider, within the bound.
No kernel may reach another device: no remote copies, remote signals or barrier semaphores. Data moves between devices by JAX's collectives and lax.ppermute only.
A program may use at most 64 MiB of HBM per device.

```python
import math
import jax
import jax.numpy as jnp
from jax import lax

D = 1024
HID = 1024
THID = 2048
TILE = 128
TILE_ROW = 4
EPT = 128
RELS = 4
SOURCES = 2048
TARGETS = 1024
TILES = 32


def draw_tile_count(key, part):
    order_key = jax.random.fold_in(key, 101)
    live_key = jax.random.fold_in(key, 202)
    amount_key = jax.random.fold_in(key, 303)
    full_key = jax.random.fold_in(key, 404)
    order = jax.random.permutation(order_key, RELS).astype(jnp.int32)
    shift_amount = order * 3 // max(RELS - 1, 1)
    keep_level = jnp.left_shift(jnp.ones((RELS,), jnp.int32), 3 - shift_amount)
    rolled = jax.random.randint(live_key, (RELS, TILES), 0, 8)
    live_mask = rolled < keep_level[:, None]
    amount = jax.random.randint(amount_key, (RELS, TILES), EPT // 2, EPT + 1)
    counts = jnp.where(live_mask, amount, 0)
    full_at = jax.random.randint(full_key, (RELS,), 0, TILES)
    position = lax.broadcasted_iota(jnp.int32, (RELS, TILES), 1)
    return jnp.where(position == full_at[:, None], EPT, counts).astype(jnp.int32)


def touch_ends(result, key, low, top_value):
    longest = result.shape.index(max(result.shape))
    spots = []
    for shift in (0, 1):
        where = [jax.random.randint(jax.random.fold_in(key, axis), (), 0, length) for axis, length in enumerate(result.shape)]
        where[longest] = (where[longest] + shift) % result.shape[longest]
        spots.append(tuple(where))
    return result.at[spots[0]].set(low).at[spots[1]].set(top_value)


def block_levels(key, shape, shards, least, high):
    gain, own = 1.0, jax.random.fold_in(key, 6)
    for axis_at, blocks in shards:
        steps = jnp.exp(jax.random.uniform(jax.random.fold_in(own, axis_at), (blocks,), jnp.float32, least / len(shards), high / len(shards)))
        gain = gain * jnp.repeat(steps, shape[axis_at] // blocks).reshape([-1 if axis == axis_at else 1 for axis in range(len(shape))])
    return gain


def noise(key, dims, deviation, limit, split=(), kind=jnp.bfloat16):
    gain = block_levels(key, dims, split, -0.22, 0.18) if split else 1.0
    entries = jax.random.normal(key, dims, jnp.float32) * deviation * gain
    return jnp.minimum(jnp.maximum(entries, -limit), limit).astype(kind)


def setup_inputs(seed: int = 0) -> dict:
    seeds = jax.random.split(jax.random.key(seed), 12)
    return {
        "src_feat": noise(seeds[0], (RELS, SOURCES, D), 1.0, 6.0, ((0, 4), (1, 8))),
        "rel_w_in": noise(seeds[1], (RELS, D, HID), D ** -0.5, 0.1875, ((0, 4), (1, 8))),
        "rel_w_out": noise(seeds[2], (RELS, HID, D), HID ** -0.5, 0.1875, ((0, 4), (1, 8))),
        "tile_source": touch_ends(jax.random.randint(seeds[3], (RELS, TILES), 0, SOURCES // TILE), jax.random.fold_in(seeds[3], 1), 0, (SOURCES // TILE) - 1).astype(jnp.int32),
        "tile_edges": touch_ends(jax.random.randint(seeds[4], (RELS, TILES, EPT), 0, TILE * TILE), jax.random.fold_in(seeds[4], 1), 0, (TILE * TILE) - 1).astype(jnp.int32),
        "tile_count": draw_tile_count(jax.random.fold_in(seeds[11], 71), 0),
        "target_feat": noise(seeds[6], (TARGETS, D), 1.0, 6.0, ((0, 32),)),
        "norm_gain": jnp.clip(jnp.exp(jax.random.uniform(seeds[7], (D,), jnp.float32, math.log(0.5), math.log(2.0))), 0.5, 2.0),
        "tgt_w_in": noise(seeds[8], (D, THID), D ** -0.5, 0.1875, ((1, 4),)),
        "tgt_w_out": noise(seeds[9], (THID, D), THID ** -0.5, 0.125, ((0, 4),)),
        "out_grad": noise(seeds[10], (TARGETS, D), 1.0, 6.0, ((0, 32),)),
    }


eps_norm = 1e-06

def silu_slope(values):
    sigma = jax.nn.sigmoid(values)
    return sigma * (1.0 + values * (1.0 - sigma))

def tile_counts(edge_codes, live_counts):
    slots = jnp.arange(edge_codes.shape[1], dtype=jnp.int32)
    live_mask = slots[None, :] < live_counts[:, None]
    lattice = jnp.arange(TILE, dtype=jnp.int32)
    target_hot = ((edge_codes // TILE)[:, :, None] == lattice[None, None, :]) & live_mask[:, :, None]
    source_hot = (edge_codes % TILE)[:, :, None] == lattice[None, None, :]
    return jnp.einsum('kes,ket->kst', source_hot.astype(jnp.float32), target_hot.astype(jnp.float32))

def reference(src_feat, rel_w_in, rel_w_out, tile_source, tile_edges, tile_count, target_feat, norm_gain, tgt_w_in, tgt_w_out, out_grad):

    def forward_one(carry_sum, inputs):
        source_rows, weight_in, weight_out, chosen, edge_codes, live_counts = inputs
        hidden_pre = jnp.dot(source_rows, weight_in, preferred_element_type=jnp.float32)
        hidden = jax.nn.silu(hidden_pre).astype(jnp.bfloat16)
        mixed = jnp.dot(hidden, weight_out, preferred_element_type=jnp.float32).astype(jnp.bfloat16)
        counts = tile_counts(edge_codes, live_counts)
        blocks = jnp.take(mixed.astype(jnp.float32).reshape(SOURCES // TILE, TILE, D), chosen, axis=0)
        contrib = jnp.einsum('kst,ksd->ktd', counts, blocks)
        contrib = contrib.reshape(TARGETS // TILE, TILE_ROW, TILE, D).sum(axis=1).reshape(TARGETS, D)
        return (carry_sum + contrib, jnp.zeros((), jnp.float32))
    inputs = (src_feat, rel_w_in, rel_w_out, tile_source, tile_edges, tile_count)
    aggregated = lax.scan(forward_one, jnp.zeros((TARGETS, D), jnp.float32), inputs)[0]
    inverse_norm = lax.rsqrt(lax.optimization_barrier(jnp.mean(aggregated * aggregated, axis=1, keepdims=True)) + eps_norm)
    gain_row = norm_gain.astype(jnp.float32)[None, :]
    normed = (aggregated * inverse_norm * gain_row).astype(jnp.bfloat16)
    target_pre = jnp.dot(normed, tgt_w_in, preferred_element_type=jnp.float32)
    target_hidden = jax.nn.silu(target_pre).astype(jnp.bfloat16)
    update = jnp.dot(target_hidden, tgt_w_out, preferred_element_type=jnp.float32)
    updated = (target_feat.astype(jnp.float32) + update).astype(jnp.bfloat16)
    grad_hidden_t = jnp.dot(out_grad, tgt_w_out.T, preferred_element_type=jnp.float32)
    grad_pre_t = (grad_hidden_t * silu_slope(target_pre)).astype(jnp.bfloat16)
    grad_normed = jnp.dot(grad_pre_t, tgt_w_in.T, preferred_element_type=jnp.float32)
    scaled = grad_normed * gain_row
    mean_term = lax.optimization_barrier(jnp.mean(aggregated * scaled, axis=1, keepdims=True))
    grad_agg = (inverse_norm * (scaled - aggregated * inverse_norm * inverse_norm * mean_term)).astype(jnp.bfloat16)

    def backward_one(inputs):
        source_rows, weight_in, weight_out, chosen, edge_codes, live_counts = inputs
        hidden_pre = jnp.dot(source_rows, weight_in, preferred_element_type=jnp.float32)
        counts = tile_counts(edge_codes, live_counts)
        per_tile = jnp.repeat(grad_agg.astype(jnp.float32).reshape(TARGETS // TILE, TILE, D), TILE_ROW, axis=0)
        contrib = jnp.einsum('kst,ktd->ksd', counts, per_tile)
        summed = jax.ops.segment_sum(contrib, chosen, num_segments=SOURCES // TILE)
        grad_mixed = summed.reshape(SOURCES, D).astype(jnp.bfloat16)
        grad_hidden = jnp.dot(grad_mixed, weight_out.T, preferred_element_type=jnp.float32)
        grad_pre = (grad_hidden * silu_slope(hidden_pre)).astype(jnp.bfloat16)
        return jnp.dot(grad_pre, weight_in.T, preferred_element_type=jnp.float32).astype(jnp.bfloat16)
    src_grad = lax.map(backward_one, inputs)
    return (updated, src_grad)
```

```python
import jax
import jax.numpy as jnp
from jax import lax
from jax.sharding import PartitionSpec as P

TILE = 128
TILE_ROW = 4


eps_norm = 1e-06


def silu_slope(values):
    sigma = jax.nn.sigmoid(values)
    return sigma * (1.0 + values * (1.0 - sigma))


def dot(a, b, ca=1, cb=0):
    return lax.dot_general(a, b, (((ca,), (cb,)), ((), ())), preferred_element_type=jnp.float32)


def swap(value, axis, size, mask):
    return lax.ppermute(value, axis, [(i, i ^ mask) for i in range(size)])


def own_counts(edge_codes, live_counts, source_ids, me, turn, own_rows, order):
    blocks = source_ids.shape[0] // TILE_ROW
    slots = edge_codes.shape[1]
    live = lax.broadcasted_iota(jnp.int32, edge_codes.shape, 1) < live_counts[:, None]
    source = source_ids[:, None] * TILE + edge_codes % TILE - me * own_rows
    source = jnp.where(live, source, -1)
    target = (edge_codes // TILE) ^ turn
    picked = jnp.asarray(order, jnp.int32) ^ me
    source = source.reshape(blocks, TILE_ROW * slots)[picked]
    target = target.reshape(blocks, TILE_ROW * slots)[picked]
    source_at = lax.broadcasted_iota(jnp.int32, (1, 1, own_rows), 2)
    target_at = lax.broadcasted_iota(jnp.int32, (1, 1, TILE), 2)
    source_hot = (source[:, :, None] == source_at).astype(jnp.bfloat16)
    target_hot = (target[:, :, None] == target_at).astype(jnp.bfloat16)
    counts = jnp.einsum("bet,bes->bts", target_hot, source_hot, preferred_element_type=jnp.float32)
    return counts.astype(jnp.bfloat16)


def make_shards(rels, devs):
    pairs = devs // 2
    evens = [2 * k for k in range(pairs)]
    odds = [2 * k + 1 for k in range(pairs)]

    def gather_dev(value):
        near = [value] + [swap(value, "dev", devs, 2 * k) for k in range(1, pairs)]
        near = jnp.concatenate(near, 0)
        return near, swap(near, "dev", devs, 1)

    def gather_rel(value):
        return jnp.concatenate([value] + [swap(value, "rel", rels, q) for q in range(1, rels)], 0)

    def reduce_rel(value):
        rows = value.shape[0] // rels
        total = value[:rows]
        for q in range(1, rels):
            piece = value[q * rows : (q + 1) * rows].astype(jnp.bfloat16)
            total = total + swap(piece, "rel", rels, q).astype(jnp.float32)
        return total

    def shards(
        src_feat,
        rel_w_in,
        rel_w_out,
        tile_source,
        tile_edges,
        tile_count,
        target_feat,
        norm_gain,
        tgt_w_in,
        tgt_w_out,
        out_grad,
    ):
        me = lax.axis_index("dev")
        rel = lax.axis_index("rel")
        own_rows = src_feat[0]
        rows = own_rows.shape[0]
        features = own_rows.shape[1]
        shard = rel_w_in.shape[1]
        gain = norm_gain[None, :]
        order = jnp.asarray(evens + odds, jnp.int32) ^ me

        in_near, in_far = gather_dev(rel_w_in[0])
        columns = own_rows.reshape(rows, devs, shard)[:, order].reshape(rows, 2, -1)
        hidden_pre = dot(columns[:, 0], in_near) + dot(columns[:, 1], in_far)
        hidden = jax.nn.silu(hidden_pre).astype(jnp.bfloat16)
        out_own, _ = lax.optimization_barrier((rel_w_out[0], in_near))
        out_near, out_far = gather_dev(out_own)

        def natural(near, far):
            both = jnp.concatenate([near, far], 0).reshape(devs, shard, -1)
            place = jnp.asarray([i // 2 + (i % 2) * pairs for i in range(devs)], jnp.int32)
            at = place[jnp.arange(devs, dtype=jnp.int32) ^ me]
            return both[at].reshape(devs * shard, -1)

        in_full = natural(in_near, in_far)
        out_full = natural(out_near, out_far)

        hidden_grad = dot(gather_rel(out_grad), tgt_w_out, 1, 1)

        sub = TILE // rels
        counts = own_counts(
            tile_edges[0], tile_count[0], tile_source[0], me, rel * sub, rows, evens + odds
        )
        counts = counts.reshape(2, pairs * TILE, rows)
        far = swap(dot(counts[1], hidden).astype(jnp.bfloat16), "dev", devs, 1)
        near = dot(counts[0], hidden) + far.astype(jnp.float32)
        total = near[:TILE]
        for k in range(1, pairs):
            piece = near[k * TILE : (k + 1) * TILE].astype(jnp.bfloat16)
            total = total + swap(piece, "dev", devs, 2 * k).astype(jnp.float32)
        agg = reduce_rel(dot(total.astype(jnp.bfloat16), out_full))

        inverse_norm = lax.rsqrt(jnp.mean(agg * agg, axis=1, keepdims=True) + eps_norm)
        normed = gather_rel((agg * inverse_norm * gain).astype(jnp.bfloat16))
        target_pre = dot(normed, tgt_w_in)
        grad_pre_t = (hidden_grad * silu_slope(target_pre)).astype(jnp.bfloat16)
        grad_normed = reduce_rel(dot(grad_pre_t, tgt_w_in, 1, 1))
        target_hidden = jax.nn.silu(target_pre).astype(jnp.bfloat16)
        scaled = grad_normed * gain
        mean_term = jnp.mean(agg * scaled, axis=1, keepdims=True)
        grad_agg = inverse_norm * (scaled - agg * inverse_norm * inverse_norm * mean_term)
        grad_agg = gather_rel(grad_agg.astype(jnp.bfloat16))
        target_hidden, grad_agg = lax.optimization_barrier((target_hidden, grad_agg))
        update = reduce_rel(dot(target_hidden, tgt_w_out))
        updated = (target_feat.astype(jnp.float32) + update).astype(jnp.bfloat16)

        back_near, back_far = gather_dev(dot(grad_agg, out_full, 1, 1).astype(jnp.bfloat16))
        grad_hidden = dot(counts[0], back_near, 0, 0) + dot(counts[1], back_far, 0, 0)
        grad_pre = (grad_hidden * silu_slope(hidden_pre)).astype(jnp.bfloat16)
        grad_source = dot(grad_pre, in_full, 1, 1)
        return (updated, grad_source.astype(jnp.bfloat16)[None])

    return shards


def solution(mesh):
    placed = (
        P("rel", "dev", None),
        P("rel", "dev", None),
        P("rel", "dev", None),
        P("rel", None),
        P("rel", None, None),
        P("rel", None),
        P(("dev", "rel"), None),
        P(),
        P(None, "rel"),
        P("rel", None),
        P(("dev", "rel"), None),
    )
    return jax.shard_map(
        make_shards(mesh.shape["rel"], mesh.shape["dev"]),
        mesh=mesh,
        in_specs=placed,
        out_specs=(P(("dev", "rel"), None), P("rel", "dev", None)),
        check_vma=False,
    )
```

```python
import jax
import jax.numpy as jnp
from jax import lax
from jax.experimental import pallas as pl
from jax.experimental.pallas import tpu as pltpu
from jax.sharding import PartitionSpec as P


TILE = 128
TILE_ROW = 4
LANES = 128


eps_norm = 1e-06


def silu_slope(values):
    sigma = jax.nn.sigmoid(values)
    return sigma * (1.0 + values * (1.0 - sigma))


def dot(a, b, ca=1, cb=0):
    return lax.dot_general(a, b, (((ca,), (cb,)), ((), ())), preferred_element_type=jnp.float32)


def swap(value, axis, size, mask):
    return lax.ppermute(value, axis, [(i, i ^ mask) for i in range(size)])


def call(body, outs, operands, scalars=0):
    flops = sum(2 * o.shape[0] * o.shape[1] * 1024 for o in outs)
    moved = sum(x.size * x.dtype.itemsize for x in list(operands) + list(outs))
    return pl.pallas_call(
        body,
        out_shape=outs,
        in_specs=[pl.BlockSpec(memory_space=pltpu.SMEM)] * scalars
        + [pl.BlockSpec(memory_space=pltpu.VMEM)] * (len(operands) - scalars),
        out_specs=[pl.BlockSpec(memory_space=pltpu.VMEM)] * len(outs),
        cost_estimate=pl.CostEstimate(flops=flops, bytes_accessed=moved, transcendentals=0),
    )(*operands)


def assemble(near, far, me, plain, turned):
    pieces = [piece for pair in zip(near, far) for piece in pair]
    count = len(pieces)
    rows, columns = pieces[0].shape
    if rows % LANES:
        both = jnp.stack(pieces, 0)[jnp.arange(count, dtype=jnp.int32) ^ me]
        both = both.reshape(count * rows, columns)
        return [both] * plain + [both.T] * turned

    def body(me_ref, *refs):
        for x in range(count):
            at = pl.ds(pl.multiple_of((me_ref[0] ^ x) * rows, rows), rows)
            value = refs[x][...]
            outs = list(refs[count:])
            if plain:
                outs.pop(0)[at, :] = value
            if turned:
                outs.pop(0)[:, at] = value.T

    outs = [jax.ShapeDtypeStruct((count * rows, columns), pieces[0].dtype)] * plain
    outs += [jax.ShapeDtypeStruct((columns, count * rows), pieces[0].dtype)] * turned
    return call(body, outs, [me[None]] + pieces, 1)


def last_step(counts, near, far, slope, weights):
    pieces = near + far

    def body(counts_ref, slope_ref, weights_ref, *refs):
        rows = jnp.concatenate([ref[...] for ref in refs[:-1]], 0)
        grad = (dot(counts_ref[...], rows) * slope_ref[...]).astype(jnp.bfloat16)
        refs[-1][...] = dot(grad, weights_ref[...]).astype(jnp.bfloat16)

    outs = [jax.ShapeDtypeStruct((counts.shape[0], weights.shape[1]), jnp.bfloat16)]
    return call(body, outs, [counts, slope, weights] + pieces)[0]


def own_counts(edge_codes, live_counts, source_ids, me, turn, own_rows, order):
    blocks = source_ids.shape[0] // TILE_ROW
    slots = edge_codes.shape[1]
    live = lax.broadcasted_iota(jnp.int32, edge_codes.shape, 1) < live_counts[:, None]
    source = source_ids[:, None] * TILE + edge_codes % TILE - me * own_rows
    source = jnp.where(live, source, -1)
    target = (edge_codes // TILE) ^ turn
    picked = jnp.asarray(order, jnp.int32) ^ me
    source = source.reshape(blocks, TILE_ROW * slots)[picked]
    target = target.reshape(blocks, TILE_ROW * slots)[picked]
    source_at = lax.broadcasted_iota(jnp.int32, (1, 1, own_rows), 2)
    target_at = lax.broadcasted_iota(jnp.int32, (1, 1, TILE), 2)
    source_hot = (source[:, :, None] == source_at).astype(jnp.bfloat16)
    target_hot = (target[:, :, None] == target_at).astype(jnp.bfloat16)
    counts = jnp.einsum("bet,bes->bts", target_hot, source_hot, preferred_element_type=jnp.float32)
    counts = counts.astype(jnp.bfloat16).reshape(-1, own_rows)
    return counts, counts.T


def make_shards(rels, devs):
    pairs = devs // 2
    evens = [2 * k for k in range(pairs)]
    odds = [2 * k + 1 for k in range(pairs)]

    def gather_dev(value):
        near = [value] + [swap(value, "dev", devs, 2 * k) for k in range(1, pairs)]
        return near, [swap(piece, "dev", devs, 1) for piece in near]

    def gather_rel(value):
        return [value] + [swap(value, "rel", rels, q) for q in range(1, rels)]

    def reduce_rel(value):
        rows = value.shape[0] // rels
        total = value[:rows]
        for q in range(1, rels):
            piece = value[q * rows : (q + 1) * rows].astype(jnp.bfloat16)
            total = total + swap(piece, "rel", rels, q).astype(jnp.float32)
        return total

    def shards(
        src_feat,
        rel_w_in,
        rel_w_out,
        tile_source,
        tile_edges,
        tile_count,
        target_feat,
        norm_gain,
        tgt_w_in,
        tgt_w_out,
        out_grad,
    ):
        me = lax.axis_index("dev")
        rel = lax.axis_index("rel")
        own_rows = src_feat[0]
        rows = own_rows.shape[0]
        shard = rel_w_in.shape[1]
        gain = norm_gain[None, :]
        order = jnp.asarray(evens + odds, jnp.int32) ^ me

        in_near, in_far = gather_dev(rel_w_in[0])
        out_near, out_far = gather_dev(rel_w_out[0])
        hidden_grad = dot(jnp.concatenate(gather_rel(out_grad), 0), tgt_w_out, 1, 1)
        sub = TILE // rels
        counts, counts_turned = own_counts(
            tile_edges[0], tile_count[0], tile_source[0], me, rel * sub, rows, evens + odds
        )
        columns = own_rows.reshape(rows, devs, shard)[:, order]
        hidden_pre = 0.0
        for k in range(pairs):
            hidden_pre = hidden_pre + dot(columns[:, k], in_near[k])
            hidden_pre = hidden_pre + dot(columns[:, pairs + k], in_far[k])
        hidden_pre, hidden_grad, counts, counts_turned = lax.optimization_barrier(
            (hidden_pre, hidden_grad, counts, counts_turned)
        )
        hidden = jax.nn.silu(hidden_pre).astype(jnp.bfloat16)

        half = pairs * TILE
        far = swap(dot(counts[half:], hidden).astype(jnp.bfloat16), "dev", devs, 1)
        near = dot(counts[:half], hidden) + far.astype(jnp.float32)
        total = near[:TILE]
        for k in range(1, pairs):
            piece = near[k * TILE : (k + 1) * TILE].astype(jnp.bfloat16)
            total = total + swap(piece, "dev", devs, 2 * k).astype(jnp.float32)
        out_full, out_turned = assemble(out_near, out_far, me, True, True)
        agg = reduce_rel(dot(total.astype(jnp.bfloat16), out_full))

        (in_turned,) = assemble(in_near, in_far, me, False, True)
        slope = silu_slope(hidden_pre)
        agg, in_turned, slope = lax.optimization_barrier((agg, in_turned, slope))
        inverse_norm = lax.rsqrt(jnp.mean(agg * agg, axis=1, keepdims=True) + eps_norm)
        normed = gather_rel((agg * inverse_norm * gain).astype(jnp.bfloat16))
        target_pre = dot(jnp.concatenate(normed, 0), tgt_w_in)
        grad_pre_t = (hidden_grad * silu_slope(target_pre)).astype(jnp.bfloat16)
        grad_normed = reduce_rel(dot(grad_pre_t, tgt_w_in, 1, 1))
        target_hidden = jax.nn.silu(target_pre).astype(jnp.bfloat16)
        scaled = grad_normed * gain
        mean_term = jnp.mean(agg * scaled, axis=1, keepdims=True)
        grad_agg = inverse_norm * (scaled - agg * inverse_norm * inverse_norm * mean_term)
        grad_agg = jnp.concatenate(gather_rel(grad_agg.astype(jnp.bfloat16)), 0)
        target_hidden, grad_agg = lax.optimization_barrier((target_hidden, grad_agg))

        back = dot(grad_agg, out_turned).astype(jnp.bfloat16)
        back_near, back_far = gather_dev(back)
        update = reduce_rel(dot(target_hidden, tgt_w_out))
        updated = (target_feat.astype(jnp.float32) + update).astype(jnp.bfloat16)
        grad_source = last_step(counts_turned, back_near, back_far, slope, in_turned)
        return (updated, grad_source[None])

    return shards


def solution(mesh):
    placed = (
        P("rel", "dev", None),
        P("rel", "dev", None),
        P("rel", "dev", None),
        P("rel", None),
        P("rel", None, None),
        P("rel", None),
        P(("dev", "rel"), None),
        P(),
        P(None, "rel"),
        P("rel", None),
        P(("dev", "rel"), None),
    )
    rels, devs = mesh.shape["rel"], mesh.shape["dev"]
    shards = make_shards(rels, devs)

    return jax.shard_map(
        shards,
        mesh=mesh,
        in_specs=placed,
        out_specs=(P(("dev", "rel"), None), P("rel", "dev", None)),
        check_vma=False,
    )
```

```python
import jax
import jax.numpy as jnp
from jax import lax
from jax.experimental import pallas as pl
from jax.experimental.pallas import tpu as pltpu
from jax.sharding import PartitionSpec as P


TILE = 128
TILE_ROW = 4
LANES = 128


eps_norm = 1e-06


def silu_slope(values):
    sigma = jax.nn.sigmoid(values)
    return sigma * (1.0 + values * (1.0 - sigma))


def dot(a, b, ca=1, cb=0):
    return lax.dot_general(a, b, (((ca,), (cb,)), ((), ())), preferred_element_type=jnp.float32)


def swap(value, axis, size, mask):
    return lax.ppermute(value, axis, [(i, i ^ mask) for i in range(size)])


def call(body, outs, operands, scalars=0):
    flops = sum(2 * o.shape[0] * o.shape[1] * 1024 for o in outs)
    moved = sum(x.size * x.dtype.itemsize for x in list(operands) + list(outs))
    return pl.pallas_call(
        body,
        out_shape=outs,
        in_specs=[pl.BlockSpec(memory_space=pltpu.SMEM)] * scalars
        + [pl.BlockSpec(memory_space=pltpu.VMEM)] * (len(operands) - scalars),
        out_specs=[pl.BlockSpec(memory_space=pltpu.VMEM)] * len(outs),
        cost_estimate=pl.CostEstimate(flops=flops, bytes_accessed=moved, transcendentals=0),
    )(*operands)


def assemble(near, far, me, plain, turned):
    pieces = [piece for pair in zip(near, far) for piece in pair]
    count = len(pieces)
    rows, columns = pieces[0].shape
    if rows % LANES:
        both = jnp.stack(pieces, 0)[jnp.arange(count, dtype=jnp.int32) ^ me]
        both = both.reshape(count * rows, columns)
        return [both] * plain + [both.T] * turned

    def body(me_ref, *refs):
        for x in range(count):
            at = pl.ds(pl.multiple_of((me_ref[0] ^ x) * rows, rows), rows)
            value = refs[x][...]
            outs = list(refs[count:])
            if plain:
                outs.pop(0)[at, :] = value
            if turned:
                outs.pop(0)[:, at] = value.T

    outs = [jax.ShapeDtypeStruct((count * rows, columns), pieces[0].dtype)] * plain
    outs += [jax.ShapeDtypeStruct((columns, count * rows), pieces[0].dtype)] * turned
    return call(body, outs, [me[None]] + pieces, 1)


def prepare(edge_codes, live_counts, source_ids, rows, me, turn, order, shard):
    own, width = rows.shape
    slots = edge_codes.shape[1]
    count = len(order)
    inside = shard % LANES == 0

    def body(scalar_ref, source_ref, live_ref, edge_ref, rows_ref, counts_ref, turned_ref, *rest):
        at, twist = scalar_ref[0], scalar_ref[1]
        slot = lax.broadcasted_iota(jnp.int32, (1, slots), 1)
        source_at = lax.broadcasted_iota(jnp.int32, (own, TILE_ROW * slots), 0)
        target_at = lax.broadcasted_iota(jnp.int32, (TILE, TILE_ROW * slots), 0)
        for i, x in enumerate(order):
            sources, targets = [], []
            for j in range(TILE_ROW):
                tile = (at ^ x) * TILE_ROW + j
                codes = edge_ref[pl.ds(tile, 1), :]
                source = source_ref[tile] * TILE + (codes & (TILE - 1)) - at * own
                sources.append(jnp.where(slot < live_ref[tile], source, -1))
                targets.append((codes // TILE) ^ twist)
            source_hot = (jnp.concatenate(sources, 1) == source_at).astype(jnp.float32)
            target_hot = (jnp.concatenate(targets, 1) == target_at).astype(jnp.float32)
            source_hot = source_hot.astype(jnp.bfloat16)
            target_hot = target_hot.astype(jnp.bfloat16)
            block = pl.ds(i * TILE, TILE)
            counts_ref[block, :] = dot(target_hot, source_hot, 1, 1).astype(jnp.bfloat16)
            turned_ref[:, block] = dot(source_hot, target_hot, 1, 1).astype(jnp.bfloat16)
            if inside:
                start = pl.multiple_of((at ^ x) * shard, shard)
                rest[0][:, i * shard : (i + 1) * shard] = rows_ref[:, pl.ds(start, shard)]

    outs = [
        jax.ShapeDtypeStruct((count * TILE, own), jnp.bfloat16),
        jax.ShapeDtypeStruct((own, count * TILE), jnp.bfloat16),
    ]
    outs += [jax.ShapeDtypeStruct((own, width), rows.dtype)] * inside
    operands = [jnp.stack([me, turn]), source_ids, live_counts, edge_codes, rows]
    results = call(body, outs, operands, 3)
    if not inside:
        picked = jnp.asarray(order, jnp.int32) ^ me
        results = [*results, rows.reshape(own, count, shard)[:, picked].reshape(own, width)]
    return results


def make_shards(rels, devs):
    pairs = devs // 2
    evens = [2 * k for k in range(pairs)]
    odds = [2 * k + 1 for k in range(pairs)]

    def gather_dev(value):
        near = [value] + [swap(value, "dev", devs, 2 * k) for k in range(1, pairs)]
        return near, [swap(piece, "dev", devs, 1) for piece in near]

    def gather_rel(value):
        return [value] + [swap(value, "rel", rels, q) for q in range(1, rels)]

    def reduce_rel(value):
        rows = value.shape[0] // rels
        total = value[:rows]
        for q in range(1, rels):
            piece = value[q * rows : (q + 1) * rows].astype(jnp.bfloat16)
            total = total + swap(piece, "rel", rels, q).astype(jnp.float32)
        return total

    def shards(
        src_feat,
        rel_w_in,
        rel_w_out,
        tile_source,
        tile_edges,
        tile_count,
        target_feat,
        norm_gain,
        tgt_w_in,
        tgt_w_out,
        out_grad,
    ):
        me = lax.axis_index("dev")
        rel = lax.axis_index("rel")
        own_rows = src_feat[0]
        shard = rel_w_in.shape[1]
        gain = norm_gain[None, :]

        in_near, in_far = gather_dev(rel_w_in[0])
        out_near, out_far = gather_dev(rel_w_out[0])
        shared_grad = gather_rel(out_grad)
        counts, counts_turned, columns = prepare(
            tile_edges[0],
            tile_count[0],
            tile_source[0],
            own_rows,
            me,
            rel * (TILE // rels),
            evens + odds,
            shard,
        )
        hidden_pre = 0.0
        for k in range(pairs):
            for at, piece in ((k, in_near[k]), (pairs + k, in_far[k])):
                hidden_pre = hidden_pre + dot(columns[:, at * shard : (at + 1) * shard], piece)
        hidden = lax.optimization_barrier(jax.nn.silu(hidden_pre).astype(jnp.bfloat16))

        half = pairs * TILE
        far = swap(dot(counts[half:], hidden).astype(jnp.bfloat16), "dev", devs, 1)
        near = dot(counts[:half], hidden) + far.astype(jnp.float32)
        total = near[:TILE]
        for k in range(1, pairs):
            piece = near[k * TILE : (k + 1) * TILE].astype(jnp.bfloat16)
            total = total + swap(piece, "dev", devs, 2 * k).astype(jnp.float32)
        out_full, out_turned = assemble(out_near, out_far, me, True, True)
        agg = reduce_rel(dot(total.astype(jnp.bfloat16), out_full))

        (in_turned,) = assemble(in_near, in_far, me, False, True)
        slope = silu_slope(hidden_pre)
        hidden_grad = dot(jnp.concatenate(shared_grad, 0), tgt_w_out, 1, 1)
        agg, in_turned, slope, hidden_grad = lax.optimization_barrier(
            (agg, in_turned, slope, hidden_grad)
        )
        inverse_norm = lax.rsqrt(jnp.mean(agg * agg, axis=1, keepdims=True) + eps_norm)
        normed = gather_rel((agg * inverse_norm * gain).astype(jnp.bfloat16))
        target_pre = dot(jnp.concatenate(normed, 0), tgt_w_in)
        grad_pre_t = (hidden_grad * silu_slope(target_pre)).astype(jnp.bfloat16)
        grad_normed = reduce_rel(dot(grad_pre_t, tgt_w_in, 1, 1))
        target_hidden = jax.nn.silu(target_pre).astype(jnp.bfloat16)
        scaled = grad_normed * gain
        mean_term = jnp.mean(agg * scaled, axis=1, keepdims=True)
        grad_agg = inverse_norm * (scaled - agg * inverse_norm * inverse_norm * mean_term)
        grad_agg = jnp.concatenate(gather_rel(grad_agg.astype(jnp.bfloat16)), 0)
        target_hidden, grad_agg = lax.optimization_barrier((target_hidden, grad_agg))

        back = dot(grad_agg, out_turned).astype(jnp.bfloat16)
        back_near, back_far = gather_dev(back)
        update = reduce_rel(dot(target_hidden, tgt_w_out))
        updated = (target_feat.astype(jnp.float32) + update).astype(jnp.bfloat16)
        grad_hidden = 0.0
        for k in range(pairs):
            for at, piece in ((k, back_near[k]), (pairs + k, back_far[k])):
                grad_hidden = grad_hidden + dot(counts_turned[:, at * TILE : (at + 1) * TILE], piece)
        grad_pre = (grad_hidden * slope).astype(jnp.bfloat16)
        grad_source = dot(grad_pre, in_turned)
        return (updated, grad_source.astype(jnp.bfloat16)[None])

    return shards


def solution(mesh):
    placed = (
        P("rel", "dev", None),
        P("rel", "dev", None),
        P("rel", "dev", None),
        P("rel", None),
        P("rel", None, None),
        P("rel", None),
        P(("dev", "rel"), None),
        P(),
        P(None, "rel"),
        P("rel", None),
        P(("dev", "rel"), None),
    )
    rels, devs = mesh.shape["rel"], mesh.shape["dev"]
    shards = make_shards(rels, devs)

    return jax.shard_map(
        shards,
        mesh=mesh,
        in_specs=placed,
        out_specs=(P(("dev", "rel"), None), P("rel", "dev", None)),
        check_vma=False,
    )
```

```python
import jax
import jax.numpy as jnp
from jax import lax
from jax.experimental import pallas as pl
from jax.experimental.pallas import tpu as pltpu
from jax.sharding import PartitionSpec as P


TILE = 128
TILE_ROW = 4
LANES = 128


eps_norm = 1e-06


def silu_slope(values):
    sigma = jax.nn.sigmoid(values)
    return sigma * (1.0 + values * (1.0 - sigma))


def dot(a, b, ca=1, cb=0):
    return lax.dot_general(a, b, (((ca,), (cb,)), ((), ())), preferred_element_type=jnp.float32)


def swap(value, axis, size, mask):
    return lax.ppermute(value, axis, [(i, i ^ mask) for i in range(size)])


def call(body, outs, operands, scalars=0):
    flops = sum(2 * o.shape[0] * o.shape[1] * 1024 for o in outs)
    moved = sum(x.size * x.dtype.itemsize for x in list(operands) + list(outs))
    return pl.pallas_call(
        body,
        out_shape=outs,
        in_specs=[pl.BlockSpec(memory_space=pltpu.SMEM)] * scalars
        + [pl.BlockSpec(memory_space=pltpu.VMEM)] * (len(operands) - scalars),
        out_specs=[pl.BlockSpec(memory_space=pltpu.VMEM)] * len(outs),
        compiler_params=pltpu.CompilerParams(vmem_limit_bytes=16 << 20),
        cost_estimate=pl.CostEstimate(flops=flops, bytes_accessed=moved, transcendentals=0),
    )(*operands)


def assemble(near, far, me, plain, turned):
    pieces = [piece for pair in zip(near, far) for piece in pair]
    count = len(pieces)
    rows, columns = pieces[0].shape
    if rows % LANES:
        both = jnp.stack(pieces, 0)[jnp.arange(count, dtype=jnp.int32) ^ me]
        both = both.reshape(count * rows, columns)
        return [both] * plain + [both.T] * turned

    def body(me_ref, *refs):
        for x in range(count):
            at = pl.ds(pl.multiple_of((me_ref[0] ^ x) * rows, rows), rows)
            value = refs[x][...]
            outs = list(refs[count:])
            if plain:
                outs.pop(0)[at, :] = value
            if turned:
                outs.pop(0)[:, at] = value.T

    outs = [jax.ShapeDtypeStruct((count * rows, columns), pieces[0].dtype)] * plain
    outs += [jax.ShapeDtypeStruct((columns, count * rows), pieces[0].dtype)] * turned
    return call(body, outs, [me[None]] + pieces, 1)


def prepare(edge_codes, live_counts, source_ids, rows, me, turn, rels, order, shard):
    own, width = rows.shape
    slots = edge_codes.shape[1]
    count = len(order)
    inside = shard % LANES == 0

    def body(me_ref, turn_ref, source_ref, live_ref, edge_ref, rows_ref, counts_ref, turned_ref, *rest):
        at, twist = me_ref[0], turn_ref[0] * (TILE // rels)
        slot = lax.broadcasted_iota(jnp.int32, (1, slots), 1)
        source_at = lax.broadcasted_iota(jnp.int32, (own, TILE_ROW * slots), 0)
        target_at = lax.broadcasted_iota(jnp.int32, (TILE, TILE_ROW * slots), 0)
        for i, x in enumerate(order):
            sources, targets = [], []
            for j in range(TILE_ROW):
                tile = (at ^ x) * TILE_ROW + j
                codes = edge_ref[pl.ds(tile, 1), :]
                source = source_ref[tile] * TILE + (codes & (TILE - 1)) - at * own
                sources.append(jnp.where(slot < live_ref[tile], source, -1))
                targets.append((codes // TILE) ^ twist)
            source_hot = (jnp.concatenate(sources, 1) == source_at).astype(jnp.float32)
            target_hot = (jnp.concatenate(targets, 1) == target_at).astype(jnp.float32)
            source_hot = source_hot.astype(jnp.bfloat16)
            target_hot = target_hot.astype(jnp.bfloat16)
            block = pl.ds(i * TILE, TILE)
            counts_ref[block, :] = dot(target_hot, source_hot, 1, 1).astype(jnp.bfloat16)
            turned_ref[:, block] = dot(source_hot, target_hot, 1, 1).astype(jnp.bfloat16)
            if inside:
                start = pl.multiple_of((at ^ x) * shard, shard)
                rest[0][:, i * shard : (i + 1) * shard] = rows_ref[:, pl.ds(start, shard)]

    outs = [
        jax.ShapeDtypeStruct((count * TILE, own), jnp.bfloat16),
        jax.ShapeDtypeStruct((own, count * TILE), jnp.bfloat16),
    ]
    outs += [jax.ShapeDtypeStruct((own, width), rows.dtype)] * inside
    operands = [me[None], turn[None], source_ids, live_counts, edge_codes, rows]
    results = call(body, outs, operands, 4)
    if not inside:
        picked = jnp.asarray(order, jnp.int32) ^ me
        results = [*results, rows.reshape(own, count, shard)[:, picked].reshape(own, width)]
    return results


def make_shards(rels, devs):
    pairs = devs // 2
    evens = [2 * k for k in range(pairs)]
    odds = [2 * k + 1 for k in range(pairs)]

    def gather_dev(value):
        near = [value] + [swap(value, "dev", devs, 2 * k) for k in range(1, pairs)]
        return near, [swap(piece, "dev", devs, 1) for piece in near]

    def gather_rel(value, masks=range(1, rels)):
        return [value] + [swap(value, "rel", rels, q) for q in masks]

    def reduce_rel(value, masks=range(1, rels)):
        rows = value.shape[0] // (1 + len(masks))
        total = value[:rows]
        for i, q in enumerate(masks, 1):
            piece = value[i * rows : (i + 1) * rows].astype(jnp.bfloat16)
            total = total + swap(piece, "rel", rels, q).astype(jnp.float32)
        return total

    def from_partner(value, me, axis):
        size = value.shape[axis] // 2
        half = lax.dynamic_slice_in_dim(value, (me & 1) * size, size, axis)
        near = swap(half, "rel", rels, 1)
        return [near, swap(near, "dev", devs, 1)]

    def shards(
        src_feat,
        rel_w_in,
        rel_w_out,
        tile_source,
        tile_edges,
        tile_count,
        target_feat,
        norm_gain,
        tgt_w_in,
        tgt_w_out,
        out_grad,
    ):
        me = lax.axis_index("dev")
        rel = lax.axis_index("rel")
        own_rows = src_feat[0]
        shard = rel_w_in.shape[1]
        gain = norm_gain[None, :]

        in_near, in_far = gather_dev(rel_w_in[0])
        out_near, out_far = gather_dev(rel_w_out[0])
        evenly = range(2, rels, 2)
        shared_grad = gather_rel(out_grad, evenly)
        more_in = from_partner(tgt_w_in, me, 1)
        more_out = from_partner(tgt_w_out, me, 0)
        counts, counts_turned, columns = prepare(
            tile_edges[0],
            tile_count[0],
            tile_source[0],
            own_rows,
            me,
            rel,
            rels,
            evens + odds,
            shard,
        )
        hidden_pre = 0.0
        for k in range(pairs):
            for at, piece in ((k, in_near[k]), (pairs + k, in_far[k])):
                hidden_pre = hidden_pre + dot(columns[:, at * shard : (at + 1) * shard], piece)
        hidden = lax.optimization_barrier(jax.nn.silu(hidden_pre).astype(jnp.bfloat16))

        half = pairs * TILE
        far = swap(dot(counts[half:], hidden).astype(jnp.bfloat16), "dev", devs, 1)
        hidden_pre, far = lax.optimization_barrier((hidden_pre, far))
        slope = silu_slope(hidden_pre)
        near = dot(counts[:half], hidden) + far.astype(jnp.float32)
        total = near[:TILE]
        for k in range(1, pairs):
            piece = near[k * TILE : (k + 1) * TILE].astype(jnp.bfloat16)
            total = total + swap(piece, "dev", devs, 2 * k).astype(jnp.float32)
        out_full, out_turned = assemble(out_near, out_far, me, True, True)
        total, more_in, more_out = lax.optimization_barrier(
            (total.astype(jnp.bfloat16), more_in, more_out)
        )
        agg = reduce_rel(dot(total, out_full))

        (in_turned,) = assemble(in_near, in_far, me, False, True)
        tgt_in = [tgt_w_in, jnp.concatenate(more_in, 1)]
        tgt_out = [tgt_w_out, jnp.concatenate(more_out, 0)]
        shared_grad = jnp.concatenate(shared_grad, 0)
        hidden_grad = [dot(shared_grad, weights, 1, 1) for weights in tgt_out]
        agg, in_turned, slope, hidden_grad, tgt_in, tgt_out = lax.optimization_barrier(
            (agg, in_turned, slope, hidden_grad, tgt_in, tgt_out)
        )
        inverse_norm = lax.rsqrt(jnp.mean(agg * agg, axis=1, keepdims=True) + eps_norm)
        normed = gather_rel((agg * inverse_norm * gain).astype(jnp.bfloat16), evenly)
        normed = jnp.concatenate(normed, 0)
        grad_normed, target_hidden = 0.0, []
        for weights, above in zip(tgt_in, hidden_grad):
            target_pre = dot(normed, weights)
            grad_pre_t = (above * silu_slope(target_pre)).astype(jnp.bfloat16)
            grad_normed = grad_normed + dot(grad_pre_t, weights, 1, 1)
            target_hidden.append(jax.nn.silu(target_pre).astype(jnp.bfloat16))
        grad_normed = reduce_rel(grad_normed, evenly)
        scaled = grad_normed * gain
        mean_term = jnp.mean(agg * scaled, axis=1, keepdims=True)
        grad_agg = inverse_norm * (scaled - agg * inverse_norm * inverse_norm * mean_term)
        grad_agg = jnp.concatenate(gather_rel(grad_agg.astype(jnp.bfloat16)), 0)
        target_hidden, grad_agg = lax.optimization_barrier((target_hidden, grad_agg))

        back = dot(grad_agg, out_turned).astype(jnp.bfloat16)
        back_near, back_far = gather_dev(back)
        update = dot(target_hidden[0], tgt_out[0]) + dot(target_hidden[1], tgt_out[1])
        update = reduce_rel(update, evenly)
        updated = (target_feat.astype(jnp.float32) + update).astype(jnp.bfloat16)
        grad_hidden = 0.0
        for k in range(pairs):
            for at, piece in ((k, back_near[k]), (pairs + k, back_far[k])):
                grad_hidden = grad_hidden + dot(counts_turned[:, at * TILE : (at + 1) * TILE], piece)
        grad_pre = lax.optimization_barrier((grad_hidden * slope).astype(jnp.bfloat16))
        grad_source = dot(grad_pre, in_turned)
        return (updated, grad_source.astype(jnp.bfloat16)[None])

    return shards


def solution(mesh):
    placed = (
        P("rel", "dev", None),
        P("rel", "dev", None),
        P("rel", "dev", None),
        P("rel", None),
        P("rel", None, None),
        P("rel", None),
        P(("dev", "rel"), None),
        P(),
        P(None, "rel"),
        P("rel", None),
        P(("dev", "rel"), None),
    )
    rels, devs = mesh.shape["rel"], mesh.shape["dev"]
    shards = make_shards(rels, devs)

    return jax.shard_map(
        shards,
        mesh=mesh,
        in_specs=placed,
        out_specs=(P(("dev", "rel"), None), P("rel", "dev", None)),
        check_vma=False,
    )
```
